32 devices in a mesh: band: 16 (over z, x, core), head: 2 (over y).
Axes of the slice: x: 2, y: 2, z: 4, core: 2. Of those that a mesh axis runs over, the one named last changes fastest.
Arguments:
- queries: bfloat16 [16, 3, 16, 512], P('band', None, None, 'head'), may hold values from -16 to 16
- attn_keys: bfloat16 [16, 3, 16, 512], P('band', None, None, 'head'), may hold values from -16 to 16
- attn_values: bfloat16 [16, 3, 16, 512], P('band', None, None, 'head'), may hold values from -16 to 16
- out_proj: bfloat16 [512, 1024], P('head'), may hold values from -0.25 to 0.25
- grad_out: bfloat16 [16, 3, 16, 1024], P('band', None, 'head'), may hold values from -24 to 24
- plane_axes: int32 [3, 2], replicated, may hold values from 0 to 2, as said below
Outputs:
- layer_out: bfloat16 [16, 3, 16, 1024], P('band', None, 'head')
- grad_queries: bfloat16 [16, 3, 16, 512], P('band', None, None, 'head')
- grad_keys: bfloat16 [16, 3, 16, 512], P('band', None, None, 'head')
- grad_values: bfloat16 [16, 3, 16, 512], P('band', None, None, 'head')
The draws below stay inside these ranges and needn't reach their ends.
Inputs may be any that keep to these rules, and one draw needn't show every extreme that they name: `plane_axes`: row p holds plane p's row axis and then its column axis, two different world axes; the three planes lack three different world axes.
All inputs are finite; a program needn't handle non-finite values.
Results may differ from the reference program's by a relative error of at most 0.018.
Values may be sent and summed in bfloat16 or wider, within the bound.
A program may use at most 64 MiB of HBM per device.

```python
import jax
import jax.numpy as jnp
from jax import lax

HEADS = 8
HEAD_DIM = 64
D = 1024
R = 16
HF = 512


def query_key_pair(base_key):
    mixed = jax.random.fold_in(base_key, 4242)
    subkeys = jax.random.split(mixed, 4)
    width = HEADS * HEAD_DIM
    shape = (R, 3, R, width)
    queries = jnp.clip(jax.random.normal(subkeys[2], shape, jnp.float32), -6.0, 6.0)
    keys_out = jnp.clip(jax.random.normal(subkeys[3], shape, jnp.float32), -6.0, 6.0)
    return (queries, keys_out)


def draw_queries(key, part):
    return query_key_pair(key)[0].astype(jnp.bfloat16)


def draw_attn_keys(key, part):
    return query_key_pair(key)[1].astype(jnp.bfloat16)


def draw_plane_axes(key, part):
    mixed = jax.random.fold_in(key, 77)
    subkeys = jax.random.split(mixed, 2)
    missing = jax.random.permutation(subkeys[0], 3).astype(jnp.int32)
    flipped = jax.random.randint(subkeys[1], (3,), 0, 2)
    first = (missing + 1) % 3
    second = (missing + 2) % 3
    row_axis = jnp.where(flipped == 1, second, first)
    column_axis = jnp.where(flipped == 1, first, second)
    return jnp.stack([row_axis, column_axis], axis=1).astype(jnp.int32)


def block_levels(own_key, dims, shards, smallest, top_value):
    factor_of, own = 1.0, jax.random.fold_in(own_key, 6)
    for position, parts in shards:
        heights = jnp.exp(jax.random.uniform(jax.random.fold_in(own, position), (parts,), jnp.float32, smallest / len(shards), top_value / len(shards)))
        factor_of = factor_of * jnp.repeat(heights, dims[position] // parts).reshape([-1 if axis == position else 1 for axis in range(len(dims))])
    return factor_of


def centred(stream_key, dims, deviation, bound, cuts=(), kind=jnp.bfloat16):
    gain = block_levels(stream_key, dims, cuts, -0.22, 0.18) if cuts else 1.0
    result = jax.random.normal(stream_key, dims, jnp.float32) * deviation * gain
    return jnp.minimum(jnp.maximum(result, -bound), bound).astype(kind)


def setup_inputs(seed: int = 0) -> dict:
    streams_of = jax.random.split(jax.random.key(seed), 7)
    queries = draw_queries(jax.random.fold_in(streams_of[6], 71), 0)
    attn_keys = draw_attn_keys(jax.random.fold_in(streams_of[6], 71), 0)
    attn_values = centred(streams_of[2], (R, 3, R, HF), 3.0, 16.0, ((0, 16), (3, 2)))
    out_proj = centred(streams_of[3], (HF, D), HF ** -0.5, 0.25, ((0, 2),))
    grad_out = centred(streams_of[4], (R, 3, R, D), 4.0, 24.0, ((0, 16), (2, 2)))
    plane_axes = draw_plane_axes(jax.random.fold_in(streams_of[6], 71), 0)
    return {"queries": queries, "attn_keys": attn_keys, "attn_values": attn_values, "out_proj": out_proj, "grad_out": grad_out, "plane_axes": plane_axes}


def partner_blocks(plane_axes):
    axis_of = jnp.concatenate([plane_axes[:, 0], plane_axes[:, 1]]).astype(jnp.int32)
    blocks = jnp.arange(6, dtype=jnp.int32)
    same = (axis_of[:, None] == axis_of[None, :]) & (blocks[:, None] != blocks[None, :])
    return jnp.sum(jnp.where(same, blocks[None, :], 0), axis=1).astype(jnp.int32)


def by_head(values):
    return values.reshape(values.shape[:-1] + (values.shape[-1] // HEAD_DIM, HEAD_DIM))


def flatten(values):
    return values.reshape(values.shape[:2] + (-1,))


def log_total(scores):
    top = jnp.max(scores, axis=-1, keepdims=True)
    return top[..., 0] + jnp.log(jnp.sum(jnp.exp(scores - top), axis=-1))


def line_scores(query_line, key_line, partner):
    factor = HEAD_DIM ** -0.5
    query_heads = by_head(query_line).astype(jnp.float32)
    key_heads = by_head(key_line).astype(jnp.float32)
    partner_keys = jnp.take(key_heads, partner, axis=0)
    cross = jnp.einsum("bahe,bche->bhac", query_heads, partner_keys) * factor
    own = jnp.einsum("bahe,bche->bhac", query_heads[:3], key_heads[:3]) * factor
    return own, cross


def forward_core(own, cross, value_line, partner):
    value_heads = by_head(value_line).astype(jnp.float32)
    partner_values = jnp.take(value_heads, partner, axis=0)
    length = own.shape[-1]
    near_scores = jnp.concatenate([own, cross[:3]], axis=-1)
    near_total = log_total(near_scores)
    near_prob = jnp.exp(near_scores - near_total[..., None]).astype(jnp.bfloat16).astype(jnp.float32)
    near_out = jnp.einsum("bhac,bche->bahe", near_prob[..., :length], value_heads[:3])
    near_out = near_out + jnp.einsum("bhac,bche->bahe", near_prob[..., length:], partner_values[:3])
    far_total = log_total(cross[3:])
    far_prob = jnp.exp(cross[3:] - far_total[..., None]).astype(jnp.bfloat16).astype(jnp.float32)
    far_out = jnp.einsum("bhac,bche->bahe", far_prob, partner_values[3:])
    return (jnp.transpose(near_total, (0, 2, 1)), flatten(near_out),
            jnp.transpose(far_total, (0, 2, 1)), flatten(far_out))


def backward_core(own, cross, line, partner):
    factor = HEAD_DIM ** -0.5
    query_line, key_line, value_line, grad_line, total_line, delta_line = line
    query_heads = by_head(query_line).astype(jnp.float32)
    key_heads = by_head(key_line).astype(jnp.float32)
    value_heads = by_head(value_line).astype(jnp.float32)
    grad_heads = by_head(grad_line).astype(jnp.float32)
    partner_keys = jnp.take(key_heads, partner, axis=0)
    partner_values = jnp.take(value_heads, partner, axis=0)
    total = jnp.transpose(total_line, (0, 2, 1))[..., None]
    delta = jnp.transpose(delta_line, (0, 2, 1))[..., None]
    cross_prob = jnp.exp(cross - total).astype(jnp.bfloat16).astype(jnp.float32)
    own_prob = jnp.exp(own - total[:3]).astype(jnp.bfloat16).astype(jnp.float32)
    cross_grad = jnp.einsum("bahe,bche->bhac", grad_heads, partner_values)
    own_grad = jnp.einsum("bahe,bche->bhac", grad_heads[:3], value_heads[:3])
    cross_step = (cross_prob * (cross_grad - delta) * factor).astype(jnp.bfloat16).astype(jnp.float32)
    own_step = (own_prob * (own_grad - delta[:3]) * factor).astype(jnp.bfloat16).astype(jnp.float32)
    grad_query = jnp.einsum("bhac,bche->bahe", cross_step, partner_keys)
    grad_query = grad_query.at[:3].add(jnp.einsum("bhac,bche->bahe", own_step, key_heads[:3]))
    toward_keys = jnp.einsum("bhac,bahe->bche", cross_step, query_heads)
    toward_values = jnp.einsum("bhac,bahe->bche", cross_prob, grad_heads)
    grad_key = jnp.take(toward_keys, partner, axis=0)
    grad_key = grad_key.at[:3].add(jnp.einsum("bhac,bahe->bche", own_step, query_heads[:3]))
    grad_value = jnp.take(toward_values, partner, axis=0)
    grad_value = grad_value.at[:3].add(jnp.einsum("bhac,bahe->bche", own_prob, grad_heads[:3]))
    return flatten(grad_query), flatten(grad_key), flatten(grad_value)


def to_lines(values):
    return jnp.concatenate([values, jnp.transpose(values, (2, 1, 0, 3))], axis=1)


def from_lines(values):
    return values[:, :3] + jnp.transpose(values[:, 3:], (2, 1, 0, 3))


def reference(queries, attn_keys, attn_values, out_proj, grad_out, plane_axes):
    partner = partner_blocks(plane_axes)
    query_lines = to_lines(queries)
    key_lines = to_lines(attn_keys)
    value_lines = to_lines(attn_values)

    def forward_one(line):
        own, cross = line_scores(line[0], line[1], partner)
        return forward_core(own, cross, line[2], partner)

    near_total, near_out, far_total, far_out = lax.map(forward_one, (query_lines, key_lines, value_lines))
    far_total = jnp.transpose(far_total, (2, 1, 0, 3))
    far_out = jnp.transpose(far_out, (2, 1, 0, 3))
    top = jnp.maximum(near_total, far_total)
    log_all = top + jnp.log(jnp.exp(near_total - top) + jnp.exp(far_total - top))
    attended = (by_head(near_out) * jnp.exp(near_total - log_all)[..., None]
                + by_head(far_out) * jnp.exp(far_total - log_all)[..., None])
    attended = attended.reshape(queries.shape).astype(jnp.bfloat16)
    layer_out = jnp.dot(attended.reshape(-1, HF), out_proj, preferred_element_type=jnp.float32)
    layer_out = layer_out.astype(jnp.bfloat16).reshape(R, 3, R, D)
    grad_attended = jnp.dot(grad_out.reshape(-1, D), out_proj.T, preferred_element_type=jnp.float32)
    grad_attended = grad_attended.astype(jnp.bfloat16).reshape(R, 3, R, HF)
    delta = jnp.sum(by_head(grad_attended).astype(jnp.float32) * by_head(attended).astype(jnp.float32), axis=-1)

    def backward_one(line):
        own, cross = line_scores(line[0], line[1], partner)
        return backward_core(own, cross, line, partner)

    grad_q, grad_k, grad_v = lax.map(backward_one, (query_lines, key_lines, value_lines, to_lines(grad_attended), to_lines(log_all), to_lines(delta)))
    return (layer_out, from_lines(grad_q).astype(jnp.bfloat16),
            from_lines(grad_k).astype(jnp.bfloat16), from_lines(grad_v).astype(jnp.bfloat16))
```

```python
import functools

import jax
import jax.numpy as jnp
from jax import lax
from jax.experimental import pallas as pl
from jax.experimental.pallas import tpu as pltpu
from jax.sharding import PartitionSpec as P

HEAD_DIM = 64
CHUNK = 16
MESH = pl.DeviceIdType.MESH
F32 = jnp.float32
BF16 = jnp.bfloat16
I32 = jnp.int32


def dot(a, b):
    return jnp.dot(a, b, preferred_element_type=F32)


def dot_bt(a, b):
    return lax.dot_general(a, b, (((1,), (1,)), ((), ())), preferred_element_type=F32)


def dot_at(a, b):
    return lax.dot_general(a, b, (((0,), (0,)), ((), ())), preferred_element_type=F32)


def iota(shape, axis):
    return lax.broadcasted_iota(I32, shape, axis)


def split3(x):
    high = x.astype(BF16)
    rest = x - high.astype(F32)
    mid = rest.astype(BF16)
    low = (rest - mid.astype(F32)).astype(BF16)
    return high, mid, low


def kernel(
    n, groups,
    q_ref, k_ref, v_ref, w_ref, go_ref, ax_ref,
    layer_ref, dq_ref, dk_ref, dv_ref,
    s1, r1, s2, r2, s3, r3, s4, r4, go_in, part_out, part_in,
    send_sem, recv_sem, head_send, head_recv,
):
    me = lax.axis_index("band")
    mine = lax.axis_index("head")
    _, planes, R, F = q_ref.shape
    rows = planes * R
    half = F // 2
    heads = F // HEAD_DIM
    width = w_ref.shape[1]
    RH = R // groups

    barrier = pltpu.get_barrier_semaphore()

    @pl.loop(1, n)
    def _(d):
        peer = lax.rem(me + d, n)
        pl.semaphore_signal(barrier, inc=1, device_id={"band": peer}, device_id_type=MESH)

    for d in range(1, groups):
        peer = lax.rem(mine + d, groups)
        pl.semaphore_signal(barrier, inc=1, device_id={"head": peer}, device_id_type=MESH)

    channels = 4 * planes

    def pack_matrix():
        r = iota((R * CHUNK, channels * R), 0)
        s = iota((R * CHUNK, channels * R), 1)
        return jnp.where(s == (r & (CHUNK - 1)) * R + (r // CHUNK), 1.0, 0.0).astype(BF16)

    def unpack_matrix():
        s = iota((channels * R, R * CHUNK), 0)
        r = iota((channels * R, R * CHUNK), 1)
        return jnp.where(s == (r & (CHUNK - 1)) * R + (r // CHUNK), 1.0, 0.0).astype(BF16)

    pack = pack_matrix()
    unpack = unpack_matrix()

    def wide(parts):
        parts = list(parts)
        return jnp.concatenate(parts + [jnp.zeros((rows, F), BF16)], axis=0)

    def narrow(a, b):
        return jnp.concatenate([a[:, :half], a[:, half:], b[:, :half], b[:, half:]], axis=0)

    def exchange_start(phase, src, dst, x):
        src[...] = dot(pack, x).astype(BF16)
        own = pl.ds(pl.multiple_of(me * CHUNK, CHUNK), CHUNK)

        @pl.loop(1, n)
        def _(d):
            copy_of(phase, src, dst, d).start()

        dst[own, :] = src[own, :]

    def copy_of(phase, src, dst, d):
        peer = lax.rem(me + d, n)
        return pltpu.make_async_remote_copy(
            src_ref=src.at[pl.ds(pl.multiple_of(peer * CHUNK, CHUNK), CHUNK)],
            dst_ref=dst.at[pl.ds(pl.multiple_of(me * CHUNK, CHUNK), CHUNK)],
            send_sem=send_sem.at[phase, d],
            recv_sem=recv_sem.at[phase, d],
            device_id={"band": peer},
            device_id_type=MESH,
        )

    def exchange_wait(phase, src, dst):
        @pl.loop(1, n)
        def _(d):
            copy_of(phase, src, dst, d).wait_recv()

        return dst[...]

    def exchange_end(phase, src, dst):
        @pl.loop(1, n)
        def _(d):
            copy_of(phase, src, dst, d).wait_send()

    def unwide(y):
        x = dot(unpack[: 3 * rows], y)
        return x[:rows], x[rows : 2 * rows], x[2 * rows :]

    def unnarrow(y):
        x = dot(unpack, y)
        a = jnp.concatenate([x[:rows], x[rows : 2 * rows]], axis=1)
        b = jnp.concatenate([x[2 * rows : 3 * rows], x[3 * rows :]], axis=1)
        return a, b

    q_row = q_ref[0].reshape(rows, F)
    k_row = k_ref[0].reshape(rows, F)
    v_row = v_ref[0].reshape(rows, F)

    def place(s):
        to = jnp.zeros_like(s)
        for w in range(groups):
            owner = lax.rem(mine - w + groups, groups)
            for p in range(planes):
                first = (w * planes + p) * RH
                inside = (s >= first) & (s < first + RH)
                to = jnp.where(inside, s - first + p * R + owner * RH, to)
        return to

    gather_rows = jnp.where(
        iota((rows, rows), 0) == place(iota((rows, rows), 1)), 1.0, 0.0
    ).astype(BF16)
    spread_rows = jnp.where(
        iota((rows, rows), 1) == place(iota((rows, rows), 0)), 1.0, 0.0
    ).astype(BF16)

    lane = iota((1, F), 1)
    lane_head = lane // HEAD_DIM
    lane_in = lane & (HEAD_DIM - 1)
    head_masks = [jnp.where(lane_head == h, 1.0, 0.0).astype(BF16) for h in range(heads)]

    def stack(x):
        return jnp.concatenate([x * head_masks[h] for h in range(heads)], axis=0)

    def fold(y):
        out = y[:rows]
        for h in range(1, heads):
            out = jnp.where(lane_head == h, y[h * rows : (h + 1) * rows], out)
        return out

    e_in, e_out = iota((F, F), 0), iota((F, F), 1)
    same_head = (e_in // HEAD_DIM) == (e_out // HEAD_DIM)
    place_in = e_in & (HEAD_DIM - 1)
    sum_all = jnp.where(same_head, 1.0, 0.0).astype(BF16)
    sum_first = jnp.where(same_head & (place_in < 3), 1.0, 0.0).astype(BF16)
    sum_second = jnp.where(same_head & (place_in >= 3) & (place_in < 6), 1.0, 0.0).astype(BF16)

    def columns(x):
        return jnp.concatenate(
            [x[:, h * HEAD_DIM : h * HEAD_DIM + 1] for h in range(heads)], axis=0
        )

    axis_of = [ax_ref[p, 0] for p in range(planes)] + [ax_ref[p, 1] for p in range(planes)]
    partner = []
    for b in range(2 * planes):
        found = jnp.int32(0)
        for c in range(2 * planes):
            if c != b:
                found = found + jnp.where(axis_of[b] == axis_of[c], jnp.int32(c), jnp.int32(0))
        partner.append(found)

    def bias_of(side):
        row, col = iota((rows, 2 * rows), 0), iota((rows, 2 * rows), 1)
        key_block = jnp.zeros_like(col)
        for b in range(1, 2 * planes):
            key_block = key_block + jnp.where(col >= b * R, 1, 0)
        block = jnp.zeros_like(row)
        for b in range(1, planes):
            block = block + jnp.where(row >= b * R, 1, 0)
        wanted = jnp.zeros_like(row)
        for b in range(planes):
            wanted = jnp.where(block == b, partner[side * planes + b], wanted)
        allowed = key_block == wanted
        if side == 0:
            allowed = allowed | (key_block == block)
        bias = jnp.where(allowed, 0.0, -1e30)
        return jnp.concatenate([bias] * heads, axis=0)

    bias_row, bias_col = bias_of(0), bias_of(1)
    scale = HEAD_DIM**-0.5

    pl.semaphore_wait(barrier, n - 1 + groups - 1)

    head_copies = []
    for d in range(1, groups):
        copy = pltpu.make_async_remote_copy(
            src_ref=go_ref.at[0],
            dst_ref=go_in.at[d - 1],
            send_sem=head_send.at[0, d],
            recv_sem=head_recv.at[0, d],
            device_id={"head": lax.rem(mine + d, groups)},
            device_id_type=MESH,
        )
        copy.start()
        head_copies.append(copy)
    exchange_start(0, s1, r1, wide([q_row, k_row, v_row]))

    for copy in head_copies:
        copy.wait_recv()
    pieces = [go_ref[0].astype(F32).reshape(planes * RH, width)]
    for d in range(1, groups):
        pieces.append(go_in[d - 1].astype(F32).reshape(planes * RH, width))
    grad_rows = jnp.concatenate(pieces, axis=0).astype(BF16)
    g_raw = dot_bt(grad_rows, w_ref[...]).astype(BF16)
    g_row = dot(gather_rows, g_raw).astype(BF16)

    q_stack_row, g_stack_row = stack(q_row), stack(g_row)

    q_col, k_col, v_col = (x.astype(BF16) for x in unwide(exchange_wait(0, s1, r1)))
    keys = jnp.concatenate([k_row, k_col], axis=0)
    values = jnp.concatenate([v_row, v_col], axis=0)

    def forward(q_stack, bias):
        scores = dot_bt(q_stack, keys) * scale + bias
        top = jnp.max(scores, axis=1, keepdims=True)
        e = jnp.exp(scores - top)
        total = jnp.sum(e, axis=1, keepdims=True)
        prob = (e * (1.0 / total)).astype(BF16)
        out = fold(dot(prob, values))
        log_sum = top + jnp.log(total)
        spread = fold(jnp.broadcast_to(log_sum, (heads * rows, F)))
        return scores, out, spread

    q_stack_col = stack(q_col)
    scores_col, far_out, far_total = forward(q_stack_col, bias_col)
    high, mid, low = split3(far_total)
    zero = jnp.zeros_like(far_total)
    stat = jnp.where(
        lane_in == 0,
        high.astype(F32),
        jnp.where(lane_in == 1, mid.astype(F32), jnp.where(lane_in == 2, low.astype(F32), zero)),
    ).astype(BF16)
    exchange_start(1, s2, r2, narrow(far_out.astype(BF16), stat))

    scores_row, near_out, near_total = forward(q_stack_row, bias_row)

    far_out, far_stat = unnarrow(exchange_wait(1, s2, r2))
    far_total = dot(far_stat.astype(BF16), sum_first)
    top = jnp.maximum(near_total, far_total)
    log_all = top + jnp.log(jnp.exp(near_total - top) + jnp.exp(far_total - top))
    attended = (
        near_out * jnp.exp(near_total - log_all) + far_out * jnp.exp(far_total - log_all)
    ).astype(BF16)
    product = g_row.astype(F32) * attended.astype(F32)
    sums = dot(jnp.concatenate(split3(product), axis=0), sum_all)
    delta = sums[:rows] + sums[rows : 2 * rows] + sums[2 * rows :]

    stat = zero
    for place_at, piece in enumerate(split3(log_all) + split3(delta)):
        stat = jnp.where(lane_in == place_at, piece.astype(F32), stat)
    exchange_start(2, s3, r3, narrow(g_row, stat.astype(BF16)))

    part = dot(dot(spread_rows, attended).astype(BF16), w_ref[...])
    part_rows = planes * RH
    layer_copies = []
    for d in range(1, groups):
        piece = part[d * part_rows : (d + 1) * part_rows]
        part_out[d - 1] = piece.reshape(planes, RH, width).astype(BF16)
        copy = pltpu.make_async_remote_copy(
            src_ref=part_out.at[d - 1],
            dst_ref=part_in.at[d - 1],
            send_sem=head_send.at[1, d],
            recv_sem=head_recv.at[1, d],
            device_id={"head": lax.rem(mine - d + groups, groups)},
            device_id_type=MESH,
        )
        copy.start()
        layer_copies.append(copy)

    def backward(scores, q_stack, g_stack, log_spread, delta_spread):
        prob = jnp.exp(scores - columns(log_spread)).astype(BF16)
        grad = dot_bt(g_stack, values)
        step = (prob.astype(F32) * (grad - columns(delta_spread)) * scale).astype(BF16)
        return fold(dot(step, keys)), dot_at(step, q_stack), dot_at(prob, g_stack)

    dq_row, dk_part, dv_part = backward(scores_row, q_stack_row, g_stack_row, log_all, delta)

    g_col, col_stat = unnarrow(exchange_wait(2, s3, r3))
    col_stat = col_stat.astype(BF16)
    log_col, delta_col = dot(col_stat, sum_first), dot(col_stat, sum_second)
    dq_col, dk_more, dv_more = backward(
        scores_col, q_stack_col, stack(g_col.astype(BF16)), log_col, delta_col
    )
    dk_all, dv_all = dk_part + dk_more, dv_part + dv_more
    exchange_start(
        3, s4, r4, wide([dq_col.astype(BF16), dk_all[rows:].astype(BF16), dv_all[rows:].astype(BF16)])
    )

    total = part[:part_rows]
    for d in range(1, groups):
        layer_copies[d - 1].wait_recv()
        total = total + part_in[d - 1].astype(F32).reshape(part_rows, width)
    layer_ref[0] = total.reshape(planes, RH, width).astype(BF16)
    for copy in head_copies + layer_copies:
        copy.wait_send()
    exchange_end(0, s1, r1)
    exchange_end(1, s2, r2)
    exchange_end(2, s3, r3)

    back_q, back_k, back_v = unwide(exchange_wait(3, s4, r4))
    dq_ref[0] = (dq_row + back_q).astype(BF16).reshape(planes, R, F)
    dk_ref[0] = (dk_all[:rows] + back_k).astype(BF16).reshape(planes, R, F)
    dv_ref[0] = (dv_all[:rows] + back_v).astype(BF16).reshape(planes, R, F)
    exchange_end(3, s4, r4)


def solution(mesh):
    n, groups = mesh.shape["band"], mesh.shape["head"]

    def body(queries, attn_keys, attn_values, out_proj, grad_out, plane_axes):
        _, planes, R, F = queries.shape
        width = out_proj.shape[1]
        vmem = pl.BlockSpec(memory_space=pltpu.VMEM)
        smem = pl.BlockSpec(memory_space=pltpu.SMEM)
        wide = pltpu.VMEM((R * CHUNK, F), BF16)
        narrow = pltpu.VMEM((R * CHUNK, F // 2), BF16)
        part = pltpu.VMEM((groups - 1, planes, R // groups, width), BF16)
        like = jax.ShapeDtypeStruct(queries.shape, BF16)
        return pl.pallas_call(
            functools.partial(kernel, n, groups),
            out_shape=(jax.ShapeDtypeStruct(grad_out.shape, BF16), like, like, like),
            in_specs=[vmem] * 5 + [smem],
            out_specs=(vmem,) * 4,
            scratch_shapes=[
                wide, wide, narrow, narrow, narrow, narrow, wide, wide, part, part, part,
                pltpu.SemaphoreType.DMA((4, n)),
                pltpu.SemaphoreType.DMA((4, n)),
                pltpu.SemaphoreType.DMA((2, groups)),
                pltpu.SemaphoreType.DMA((2, groups)),
            ],
            compiler_params=pltpu.CompilerParams(
                collective_id=0, has_side_effects=True, vmem_limit_bytes=60 * 1024 * 1024
            ),
        )(queries, attn_keys, attn_values, out_proj, grad_out, plane_axes)

    rows = P("band", None, None, "head")
    cols = P("band", None, "head", None)
    return jax.shard_map(
        body,
        mesh=mesh,
        in_specs=(rows, rows, rows, P("head", None), cols, P()),
        out_specs=(cols, rows, rows, rows),
        check_vma=False,
    )
```

```python
import functools

import jax
import jax.numpy as jnp
from jax import lax
from jax.experimental import pallas as pl
from jax.experimental.pallas import tpu as pltpu
from jax.sharding import PartitionSpec as P

HEAD_DIM = 64
CHUNK = 16
MESH = pl.DeviceIdType.MESH
F32 = jnp.float32
BF16 = jnp.bfloat16
I32 = jnp.int32


def dot(a, b):
    return jnp.dot(a, b, preferred_element_type=F32)


def dot_bt(a, b):
    return lax.dot_general(a, b, (((1,), (1,)), ((), ())), preferred_element_type=F32)


def dot_at(a, b):
    return lax.dot_general(a, b, (((0,), (0,)), ((), ())), preferred_element_type=F32)


def iota(shape, axis):
    return lax.broadcasted_iota(I32, shape, axis)


def split3(x):
    high = x.astype(BF16)
    rest = x - high.astype(F32)
    mid = rest.astype(BF16)
    low = (rest - mid.astype(F32)).astype(BF16)
    return high, mid, low


def kernel(
    n, groups,
    q_hbm, k_hbm, v_hbm, w_hbm, go_hbm, ax_hbm,
    layer_ref, dq_ref, dk_ref, dv_ref,
    q_ref, k_ref, v_ref, w_ref, go_ref, ax_ref,
    s1, r1, s2, r2, s3, r3, s4, r4, go_in, part_out, part_in,
    send_sem, recv_sem, head_send, head_recv, load_sem,
):
    me = lax.axis_index("band")
    mine = lax.axis_index("head")
    _, planes, R, F = q_ref.shape
    rows = planes * R
    half = F // 2
    heads = F // HEAD_DIM
    width = w_ref.shape[1]
    RH = R // groups

    barrier = pltpu.get_barrier_semaphore()

    @pl.loop(1, n)
    def _(d):
        peer = lax.rem(me + d, n)
        pl.semaphore_signal(barrier, inc=1, device_id={"band": peer}, device_id_type=MESH)

    for d in range(1, groups):
        peer = lax.rem(mine + d, groups)
        pl.semaphore_signal(barrier, inc=1, device_id={"head": peer}, device_id_type=MESH)

    loads = [
        pltpu.make_async_copy(src, dst, load_sem.at[at])
        for at, (src, dst) in enumerate(
            [
                (q_hbm, q_ref), (k_hbm, k_ref), (v_hbm, v_ref),
                (ax_hbm, ax_ref), (go_hbm, go_ref), (w_hbm, w_ref),
            ]
        )
    ]
    for load in loads:
        load.start()

    channels = 4 * planes

    def pack_matrix():
        r = iota((R * CHUNK, channels * R), 0)
        s = iota((R * CHUNK, channels * R), 1)
        return jnp.where(s == (r & (CHUNK - 1)) * R + (r // CHUNK), 1.0, 0.0).astype(BF16)

    def unpack_matrix():
        s = iota((channels * R, R * CHUNK), 0)
        r = iota((channels * R, R * CHUNK), 1)
        return jnp.where(s == (r & (CHUNK - 1)) * R + (r // CHUNK), 1.0, 0.0).astype(BF16)

    pack = pack_matrix()
    unpack = unpack_matrix()

    def wide(parts):
        parts = list(parts)
        return jnp.concatenate(parts + [jnp.zeros((rows, F), BF16)], axis=0)

    def narrow(a, b):
        return jnp.concatenate([a[:, :half], a[:, half:], b[:, :half], b[:, half:]], axis=0)

    def exchange_start(phase, src, dst, x):
        if x is not None:
            src[...] = dot(pack, x).astype(BF16)
        own = pl.ds(pl.multiple_of(me * CHUNK, CHUNK), CHUNK)

        @pl.loop(0, n - 1)
        def _(i):
            away = (i + 1) // 2
            d = n // 2 + away * (1 - 2 * lax.rem(i, 2))
            peer = lax.rem(me + d, n)
            pltpu.make_async_remote_copy(
                src_ref=src.at[pl.ds(pl.multiple_of(peer * CHUNK, CHUNK), CHUNK)],
                dst_ref=dst.at[own],
                send_sem=send_sem.at[phase],
                recv_sem=recv_sem.at[phase],
                device_id={"band": peer},
                device_id_type=MESH,
            ).start()

        dst[own, :] = src[own, :]

    def all_copies(phase, src, dst):
        others = pl.ds(0, (n - 1) * CHUNK)
        return pltpu.make_async_remote_copy(
            src_ref=src.at[others],
            dst_ref=dst.at[others],
            send_sem=send_sem.at[phase],
            recv_sem=recv_sem.at[phase],
            device_id={"band": lax.rem(me + 1, n)},
            device_id_type=MESH,
        )

    def exchange_wait(phase, src, dst):
        all_copies(phase, src, dst).wait_recv()
        return dst[...]

    def exchange_end(phase, src, dst):
        all_copies(phase, src, dst).wait_send()

    def unwide(y):
        x = dot(unpack[: 3 * rows], y)
        return x[:rows], x[rows : 2 * rows], x[2 * rows :]

    def unnarrow(y):
        x = dot(unpack, y)
        a = jnp.concatenate([x[:rows], x[rows : 2 * rows]], axis=1)
        b = jnp.concatenate([x[2 * rows : 3 * rows], x[3 * rows :]], axis=1)
        return a, b


    def place(s):
        to = jnp.zeros_like(s)
        for w in range(groups):
            owner = lax.rem(mine - w + groups, groups)
            for p in range(planes):
                first = (w * planes + p) * RH
                inside = (s >= first) & (s < first + RH)
                to = jnp.where(inside, s - first + p * R + owner * RH, to)
        return to

    gather_rows = jnp.where(
        iota((rows, rows), 0) == place(iota((rows, rows), 1)), 1.0, 0.0
    ).astype(BF16)
    spread_rows = jnp.where(
        iota((rows, rows), 1) == place(iota((rows, rows), 0)), 1.0, 0.0
    ).astype(BF16)

    lane = iota((1, F), 1)
    lane_head = lane // HEAD_DIM
    lane_in = lane & (HEAD_DIM - 1)
    head_masks = [jnp.where(lane_head == h, 1.0, 0.0).astype(BF16) for h in range(heads)]

    def stack(x):
        return jnp.concatenate([x * head_masks[h] for h in range(heads)], axis=0)

    def fold(y):
        out = y[:rows]
        for h in range(1, heads):
            out = jnp.where(lane_head == h, y[h * rows : (h + 1) * rows], out)
        return out

    e_in, e_out = iota((F, F), 0), iota((F, F), 1)
    same_head = (e_in // HEAD_DIM) == (e_out // HEAD_DIM)
    place_in = e_in & (HEAD_DIM - 1)
    sum_all = jnp.where(same_head, 1.0, 0.0).astype(BF16)
    sum_first = jnp.where(same_head & (place_in < 3), 1.0, 0.0).astype(BF16)
    sum_second = jnp.where(same_head & (place_in >= 3) & (place_in < 6), 1.0, 0.0).astype(BF16)

    def columns(x):
        return jnp.concatenate(
            [x[:, h * HEAD_DIM : h * HEAD_DIM + 1] for h in range(heads)], axis=0
        )

    for load in loads[:4]:
        load.wait()
    axis_of = [ax_ref[0, p] for p in range(planes)] + [ax_ref[1, p] for p in range(planes)]
    partner = []
    for b in range(2 * planes):
        found = jnp.int32(0)
        for c in range(2 * planes):
            if c != b:
                found = found + jnp.where(axis_of[b] == axis_of[c], jnp.int32(c), jnp.int32(0))
        partner.append(found)

    def bias_of(side):
        row, col = iota((rows, 2 * rows), 0), iota((rows, 2 * rows), 1)
        key_block = jnp.zeros_like(col)
        for b in range(1, 2 * planes):
            key_block = key_block + jnp.where(col >= b * R, 1, 0)
        block = jnp.zeros_like(row)
        for b in range(1, planes):
            block = block + jnp.where(row >= b * R, 1, 0)
        wanted = jnp.zeros_like(row)
        for b in range(planes):
            wanted = jnp.where(block == b, partner[side * planes + b], wanted)
        allowed = key_block == wanted
        if side == 0:
            allowed = allowed | (key_block == block)
        bias = jnp.where(allowed, 0.0, -1e30)
        return jnp.concatenate([bias] * heads, axis=0)

    bias_row, bias_col = bias_of(0), bias_of(1)
    scale = HEAD_DIM**-0.5

    q_row = q_ref[0].reshape(rows, F)
    k_row = k_ref[0].reshape(rows, F)
    v_row = v_ref[0].reshape(rows, F)
    s1[...] = dot(pack, wide([q_row, k_row, v_row])).astype(BF16)
    q_stack_row = stack(q_row)

    pl.semaphore_wait(barrier, n - 1 + groups - 1)

    head_copies = []
    for d in range(1, groups):
        copy = pltpu.make_async_remote_copy(
            src_ref=go_hbm.at[0],
            dst_ref=go_in.at[d - 1],
            send_sem=head_send.at[0, d - 1],
            recv_sem=head_recv.at[0, d - 1],
            device_id={"head": lax.rem(mine + d, groups)},
            device_id_type=MESH,
        )
        copy.start()
        head_copies.append(copy)
    exchange_start(0, s1, r1, None)

    for load in loads[4:]:
        load.wait()
    for copy in head_copies:
        copy.wait_recv()
    pieces = [go_ref[0].astype(F32).reshape(planes * RH, width)]
    for d in range(1, groups):
        pieces.append(go_in[d - 1].astype(F32).reshape(planes * RH, width))
    grad_rows = jnp.concatenate(pieces, axis=0).astype(BF16)
    g_raw = dot_bt(grad_rows, w_ref[...]).astype(BF16)
    g_row = dot(gather_rows, g_raw).astype(BF16)

    g_stack_row = stack(g_row)

    q_col, k_col, v_col = (x.astype(BF16) for x in unwide(exchange_wait(0, s1, r1)))
    keys = jnp.concatenate([k_row, k_col], axis=0)
    values = jnp.concatenate([v_row, v_col], axis=0)

    def forward(q_stack, bias):
        scores = dot_bt(q_stack, keys) * scale + bias
        top = jnp.max(scores, axis=1, keepdims=True)
        e = jnp.exp(scores - top)
        total = jnp.sum(e, axis=1, keepdims=True)
        prob = (e * (1.0 / total)).astype(BF16)
        out = fold(dot(prob, values))
        log_sum = top + jnp.log(total)
        spread = fold(jnp.broadcast_to(log_sum, (heads * rows, F)))
        return scores, out, spread

    q_stack_col = stack(q_col)
    scores_col, far_out, far_total = forward(q_stack_col, bias_col)
    high, mid, low = split3(far_total)
    zero = jnp.zeros_like(far_total)
    stat = jnp.where(
        lane_in == 0,
        high.astype(F32),
        jnp.where(lane_in == 1, mid.astype(F32), jnp.where(lane_in == 2, low.astype(F32), zero)),
    ).astype(BF16)
    exchange_start(1, s2, r2, narrow(far_out.astype(BF16), stat))

    scores_row, near_out, near_total = forward(q_stack_row, bias_row)
    product_row = dot_bt(g_stack_row, values)

    far_out, far_stat = unnarrow(exchange_wait(1, s2, r2))
    far_total = dot(far_stat.astype(BF16), sum_first)
    top = jnp.maximum(near_total, far_total)
    log_all = top + jnp.log(jnp.exp(near_total - top) + jnp.exp(far_total - top))
    attended = (
        near_out * jnp.exp(near_total - log_all) + far_out * jnp.exp(far_total - log_all)
    ).astype(BF16)
    product = g_row.astype(F32) * attended.astype(F32)
    sums = dot(jnp.concatenate(split3(product), axis=0), sum_all)
    delta = sums[:rows] + sums[rows : 2 * rows] + sums[2 * rows :]

    stat = zero
    for place_at, piece in enumerate(split3(log_all) + split3(delta)):
        stat = jnp.where(lane_in == place_at, piece.astype(F32), stat)
    exchange_start(2, s3, r3, narrow(g_row, stat.astype(BF16)))

    part = dot(dot(spread_rows, attended).astype(BF16), w_ref[...])
    part_rows = planes * RH
    layer_copies = []
    for d in range(1, groups):
        piece = part[d * part_rows : (d + 1) * part_rows]
        part_out[d - 1] = piece.reshape(planes, RH, width).astype(BF16)
        copy = pltpu.make_async_remote_copy(
            src_ref=part_out.at[d - 1],
            dst_ref=part_in.at[d - 1],
            send_sem=head_send.at[1, d - 1],
            recv_sem=head_recv.at[1, d - 1],
            device_id={"head": lax.rem(mine - d + groups, groups)},
            device_id_type=MESH,
        )
        copy.start()
        layer_copies.append(copy)

    def backward(scores, q_stack, g_stack, grad, log_spread, delta_spread):
        prob = jnp.exp(scores - columns(log_spread)).astype(BF16)
        step = (prob.astype(F32) * (grad - columns(delta_spread)) * scale).astype(BF16)
        return fold(dot(step, keys)), dot_at(step, q_stack), dot_at(prob, g_stack)

    dq_row, dk_part, dv_part = backward(
        scores_row, q_stack_row, g_stack_row, product_row, log_all, delta
    )

    g_col, col_stat = unnarrow(exchange_wait(2, s3, r3))
    col_stat = col_stat.astype(BF16)
    log_col, delta_col = dot(col_stat, sum_first), dot(col_stat, sum_second)
    g_stack_col = stack(g_col.astype(BF16))
    dq_col, dk_more, dv_more = backward(
        scores_col, q_stack_col, g_stack_col, dot_bt(g_stack_col, values), log_col, delta_col
    )
    dk_all, dv_all = dk_part + dk_more, dv_part + dv_more
    exchange_start(
        3, s4, r4, wide([dq_col.astype(BF16), dk_all[rows:].astype(BF16), dv_all[rows:].astype(BF16)])
    )

    total = part[:part_rows]
    for d in range(1, groups):
        layer_copies[d - 1].wait_recv()
        total = total + part_in[d - 1].astype(F32).reshape(part_rows, width)
    layer_ref[0] = total.reshape(planes, RH, width).astype(BF16)
    for copy in head_copies + layer_copies:
        copy.wait_send()
    exchange_end(0, s1, r1)
    exchange_end(1, s2, r2)
    exchange_end(2, s3, r3)

    back_q, back_k, back_v = unwide(exchange_wait(3, s4, r4))
    dq_ref[0] = (dq_row + back_q).astype(BF16).reshape(planes, R, F)
    dk_ref[0] = (dk_all[:rows] + back_k).astype(BF16).reshape(planes, R, F)
    dv_ref[0] = (dv_all[:rows] + back_v).astype(BF16).reshape(planes, R, F)
    exchange_end(3, s4, r4)


def store_kernel(*refs):
    sources, targets, sem = refs[:4], refs[4:8], refs[8]
    copies = [
        pltpu.make_async_copy(src, dst, sem.at[at])
        for at, (src, dst) in enumerate(zip(sources, targets))
    ]
    for copy in copies:
        copy.start()
    for copy in copies:
        copy.wait()


def solution(mesh):
    n, groups = mesh.shape["band"], mesh.shape["head"]

    def body(queries, attn_keys, attn_values, out_proj, grad_out, plane_axes):
        _, planes, R, F = queries.shape
        width = out_proj.shape[1]
        whole = pl.BlockSpec(memory_space=pl.ANY)
        vmem = pl.BlockSpec(memory_space=pltpu.VMEM)
        wide = pltpu.VMEM((R * CHUNK, F), BF16)
        narrow = pltpu.VMEM((R * CHUNK, F // 2), BF16)
        part = pltpu.VMEM((groups - 1, planes, R // groups, width), BF16)
        shapes = [grad_out.shape] + [queries.shape] * 3
        results = pl.pallas_call(
            functools.partial(kernel, n, groups),
            out_shape=tuple(pltpu.VMEM(shape, BF16) for shape in shapes),
            in_specs=[whole] * 6,
            out_specs=(vmem,) * 4,
            scratch_shapes=[
                pltpu.VMEM(queries.shape, BF16),
                pltpu.VMEM(queries.shape, BF16),
                pltpu.VMEM(queries.shape, BF16),
                pltpu.VMEM(out_proj.shape, BF16),
                pltpu.VMEM(grad_out.shape, BF16),
                pltpu.SMEM(plane_axes.shape[::-1], I32),
                wide, wide, narrow, narrow, narrow, narrow, wide, wide, part, part, part,
                pltpu.SemaphoreType.DMA((4,)),
                pltpu.SemaphoreType.DMA((4,)),
                pltpu.SemaphoreType.DMA((2, groups - 1)),
                pltpu.SemaphoreType.DMA((2, groups - 1)),
                pltpu.SemaphoreType.DMA((6,)),
            ],
            compiler_params=pltpu.CompilerParams(
                collective_id=0, has_side_effects=True, vmem_limit_bytes=56 * 1024 * 1024
            ),
        )(queries, attn_keys, attn_values, out_proj, grad_out, plane_axes.T)
        return pl.pallas_call(
            store_kernel,
            out_shape=tuple(jax.ShapeDtypeStruct(shape, BF16) for shape in shapes),
            in_specs=[vmem] * 4,
            out_specs=(whole,) * 4,
            scratch_shapes=[pltpu.SemaphoreType.DMA((4,))],
        )(*[pltpu.with_memory_space_constraint(r, pltpu.VMEM) for r in results])

    rows = P("band", None, None, "head")
    cols = P("band", None, "head", None)
    return jax.shard_map(
        body,
        mesh=mesh,
        in_specs=(rows, rows, rows, P("head", None), cols, P()),
        out_specs=(cols, rows, rows, rows),
        check_vma=False,
    )
```

```python
import functools

import jax
import jax.numpy as jnp
from jax import lax
from jax.experimental import pallas as pl
from jax.experimental.pallas import tpu as pltpu
from jax.sharding import PartitionSpec as P

HEAD_DIM = 64
CHUNK = 16
MESH = pl.DeviceIdType.MESH
F32 = jnp.float32
BF16 = jnp.bfloat16
I32 = jnp.int32


def dot(a, b):
    return jnp.dot(a, b, preferred_element_type=F32)


def dot_bt(a, b):
    return lax.dot_general(a, b, (((1,), (1,)), ((), ())), preferred_element_type=F32)


def dot_at(a, b):
    return lax.dot_general(a, b, (((0,), (0,)), ((), ())), preferred_element_type=F32)


def iota(shape, axis):
    return lax.broadcasted_iota(I32, shape, axis)


def split3(x):
    high = x.astype(BF16)
    rest = x - high.astype(F32)
    mid = rest.astype(BF16)
    low = (rest - mid.astype(F32)).astype(BF16)
    return high, mid, low


def kernel(
    n, groups,
    q_hbm, k_hbm, v_hbm, w_hbm, go_hbm, ax_hbm,
    layer_ref, dq_ref, dk_ref, dv_ref,
    q_ref, k_ref, v_ref, w_ref, go_ref, ax_ref,
    s1, r1, s2, r2, s3, r3, s4, r4, go_in, part_out, part_in,
    send_sem, recv_sem, head_send, head_recv, load_sem,
):
    me = lax.axis_index("band")
    mine = lax.axis_index("head")
    _, planes, R, F = q_ref.shape
    rows = planes * R
    half = F // 2
    heads = F // HEAD_DIM
    width = w_ref.shape[1]
    RH = R // groups

    barrier = pltpu.get_barrier_semaphore()

    @pl.loop(1, n)
    def _(d):
        peer = lax.rem(me + d, n)
        pl.semaphore_signal(barrier, inc=1, device_id={"band": peer}, device_id_type=MESH)

    for d in range(1, groups):
        peer = lax.rem(mine + d, groups)
        pl.semaphore_signal(barrier, inc=1, device_id={"head": peer}, device_id_type=MESH)

    loads = [
        pltpu.make_async_copy(src, dst, load_sem.at[at])
        for at, (src, dst) in enumerate(
            [
                (q_hbm, q_ref), (k_hbm, k_ref), (v_hbm, v_ref),
                (ax_hbm, ax_ref), (go_hbm, go_ref), (w_hbm, w_ref),
            ]
        )
    ]
    for load in loads:
        load.start()

    channels = 4 * planes

    def pack_matrix():
        r = iota((R * CHUNK, channels * R), 0)
        s = iota((R * CHUNK, channels * R), 1)
        return jnp.where(s == (r & (CHUNK - 1)) * R + (r // CHUNK), 1.0, 0.0).astype(BF16)

    def unpack_matrix():
        s = iota((channels * R, R * CHUNK), 0)
        r = iota((channels * R, R * CHUNK), 1)
        return jnp.where(s == (r & (CHUNK - 1)) * R + (r // CHUNK), 1.0, 0.0).astype(BF16)

    pack = pack_matrix()
    unpack = unpack_matrix()

    def wide(parts):
        parts = list(parts)
        return jnp.concatenate(parts + [jnp.zeros((rows, F), BF16)], axis=0)

    def narrow(a, b):
        return jnp.concatenate([a[:, :half], a[:, half:], b[:, :half], b[:, half:]], axis=0)

    def exchange_start(phase, src, dst, x):
        if x is not None:
            src[...] = dot(pack, x).astype(BF16)
        own = pl.ds(pl.multiple_of(me * CHUNK, CHUNK), CHUNK)

        @pl.loop(0, n - 1)
        def _(i):
            away = (i + 1) // 2
            d = n // 2 + away * (1 - 2 * lax.rem(i, 2))
            peer = lax.rem(me + d, n)
            pltpu.make_async_remote_copy(
                src_ref=src.at[pl.ds(pl.multiple_of(peer * CHUNK, CHUNK), CHUNK)],
                dst_ref=dst.at[own],
                send_sem=send_sem.at[phase],
                recv_sem=recv_sem.at[phase],
                device_id={"band": peer},
                device_id_type=MESH,
            ).start()

        dst[own, :] = src[own, :]

    def all_copies(phase, src, dst):
        others = pl.ds(0, (n - 1) * CHUNK)
        return pltpu.make_async_remote_copy(
            src_ref=src.at[others],
            dst_ref=dst.at[others],
            send_sem=send_sem.at[phase],
            recv_sem=recv_sem.at[phase],
            device_id={"band": lax.rem(me + 1, n)},
            device_id_type=MESH,
        )

    def exchange_wait(phase, src, dst):
        all_copies(phase, src, dst).wait_recv()
        return dst[...]

    def exchange_end(phase, src, dst):
        all_copies(phase, src, dst).wait_send()

    def unwide(y):
        x = dot(unpack[: 3 * rows], y)
        return x[:rows], x[rows : 2 * rows], x[2 * rows :]

    def unnarrow(y):
        x = dot(unpack, y)
        a = jnp.concatenate([x[:rows], x[rows : 2 * rows]], axis=1)
        b = jnp.concatenate([x[2 * rows : 3 * rows], x[3 * rows :]], axis=1)
        return a, b


    def place(s):
        to = jnp.zeros_like(s)
        for w in range(groups):
            owner = lax.rem(mine - w + groups, groups)
            for p in range(planes):
                first = (w * planes + p) * RH
                inside = (s >= first) & (s < first + RH)
                to = jnp.where(inside, s - first + p * R + owner * RH, to)
        return to

    gather_rows = jnp.where(
        iota((rows, rows), 0) == place(iota((rows, rows), 1)), 1.0, 0.0
    ).astype(BF16)
    spread_rows = jnp.where(
        iota((rows, rows), 1) == place(iota((rows, rows), 0)), 1.0, 0.0
    ).astype(BF16)

    lane = iota((1, F), 1)
    lane_head = lane // HEAD_DIM
    lane_in = lane & (HEAD_DIM - 1)
    head_masks = [jnp.where(lane_head == h, 1.0, 0.0).astype(BF16) for h in range(heads)]

    def stack(x):
        return jnp.concatenate([x * head_masks[h] for h in range(heads)], axis=0)

    def fold(y):
        out = y[:rows]
        for h in range(1, heads):
            out = jnp.where(lane_head == h, y[h * rows : (h + 1) * rows], out)
        return out

    e_in, e_out = iota((F, F), 0), iota((F, F), 1)
    same_head = (e_in // HEAD_DIM) == (e_out // HEAD_DIM)
    place_in = e_in & (HEAD_DIM - 1)
    sum_all = jnp.where(same_head, 1.0, 0.0).astype(BF16)
    sum_first = jnp.where(same_head & (place_in < 3), 1.0, 0.0).astype(BF16)
    sum_second = jnp.where(same_head & (place_in >= 3) & (place_in < 6), 1.0, 0.0).astype(BF16)
    sum_third = jnp.where(same_head & (place_in >= 6) & (place_in < 9), 1.0, 0.0).astype(BF16)

    def columns(x):
        return jnp.concatenate(
            [x[:, h * HEAD_DIM : h * HEAD_DIM + 1] for h in range(heads)], axis=0
        )

    for load in loads[:4]:
        load.wait()
    axis_of = [ax_ref[0, p] for p in range(planes)] + [ax_ref[1, p] for p in range(planes)]
    partner = []
    for b in range(2 * planes):
        found = jnp.int32(0)
        for c in range(2 * planes):
            if c != b:
                found = found + jnp.where(axis_of[b] == axis_of[c], jnp.int32(c), jnp.int32(0))
        partner.append(found)

    def bias_of(side):
        row, col = iota((rows, 2 * rows), 0), iota((rows, 2 * rows), 1)
        key_block = jnp.zeros_like(col)
        for b in range(1, 2 * planes):
            key_block = key_block + jnp.where(col >= b * R, 1, 0)
        block = jnp.zeros_like(row)
        for b in range(1, planes):
            block = block + jnp.where(row >= b * R, 1, 0)
        wanted = jnp.zeros_like(row)
        for b in range(planes):
            wanted = jnp.where(block == b, partner[side * planes + b], wanted)
        allowed = key_block == wanted
        if side == 0:
            allowed = allowed | (key_block == block)
        bias = jnp.where(allowed, 0.0, -1e30)
        return jnp.concatenate([bias] * heads, axis=0)

    bias_row, bias_col = bias_of(0), bias_of(1)
    scale = HEAD_DIM**-0.5

    q_row = q_ref[0].reshape(rows, F)
    k_row = k_ref[0].reshape(rows, F)
    v_row = v_ref[0].reshape(rows, F)
    s1[...] = dot(pack, wide([q_row, k_row, v_row])).astype(BF16)
    q_stack_row = stack(q_row)

    pl.semaphore_wait(barrier, n - 1 + groups - 1)

    head_copies = []
    for d in range(1, groups):
        copy = pltpu.make_async_remote_copy(
            src_ref=go_hbm.at[0],
            dst_ref=go_in.at[d - 1],
            send_sem=head_send.at[0, d - 1],
            recv_sem=head_recv.at[0, d - 1],
            device_id={"head": lax.rem(mine + d, groups)},
            device_id_type=MESH,
        )
        copy.start()
        head_copies.append(copy)
    exchange_start(0, s1, r1, None)

    for load in loads[4:]:
        load.wait()
    for copy in head_copies:
        copy.wait_recv()
    pieces = [go_ref[0].astype(F32).reshape(planes * RH, width)]
    for d in range(1, groups):
        pieces.append(go_in[d - 1].astype(F32).reshape(planes * RH, width))
    grad_rows = jnp.concatenate(pieces, axis=0).astype(BF16)
    g_raw = dot_bt(grad_rows, w_ref[...]).astype(BF16)
    g_row = dot(gather_rows, g_raw).astype(BF16)

    exchange_start(1, s2, r2, narrow(g_row, jnp.zeros_like(g_row)))
    g_stack_row = stack(g_row)

    q_col, k_col, v_col = (x.astype(BF16) for x in unwide(exchange_wait(0, s1, r1)))
    keys = jnp.concatenate([k_row, k_col], axis=0)
    values = jnp.concatenate([v_row, v_col], axis=0)

    def forward(q_stack, bias):
        scores = dot_bt(q_stack, keys) * scale + bias
        top = jnp.max(scores, axis=1, keepdims=True)
        e = jnp.exp(scores - top)
        total = jnp.sum(e, axis=1, keepdims=True)
        prob = (e * (1.0 / total)).astype(BF16)
        out = fold(dot(prob, values))
        log_sum = top + jnp.log(total)
        spread = fold(jnp.broadcast_to(log_sum, (heads * rows, F)))
        return scores, out, spread

    q_stack_col = stack(q_col)
    scores_col, far_out, far_total = forward(q_stack_col, bias_col)
    scores_row, near_out, near_total = forward(q_stack_row, bias_row)
    far_out = far_out.astype(BF16)

    def head_sums(product):
        sums = dot(jnp.concatenate(split3(product), axis=0), sum_all)
        return sums[:rows] + sums[rows : 2 * rows] + sums[2 * rows :]

    near_delta = head_sums(g_row.astype(F32) * near_out)
    stat = jnp.zeros_like(far_total)
    for at, piece in enumerate(split3(far_total) + split3(near_total) + split3(near_delta)):
        stat = jnp.where(lane_in == at, piece.astype(F32), stat)
    exchange_start(2, s3, r3, narrow(far_out, stat.astype(BF16)))

    product_row = dot_bt(g_stack_row, values)
    g_col = unnarrow(exchange_wait(1, s2, r2))[0].astype(BF16)
    g_stack_col = stack(g_col)
    product_col = dot_bt(g_stack_col, values)
    own_delta = head_sums(g_col.astype(F32) * far_out.astype(F32))

    def combine(near_total, near_delta, far_total, far_delta):
        top = jnp.maximum(near_total, far_total)
        log_all = top + jnp.log(jnp.exp(near_total - top) + jnp.exp(far_total - top))
        near_weight, far_weight = jnp.exp(near_total - log_all), jnp.exp(far_total - log_all)
        delta = near_weight * near_delta + far_weight * far_delta
        return log_all, delta, near_weight, far_weight

    row_far_out, stat = unnarrow(exchange_wait(2, s3, r3))
    stat = stat.astype(BF16)
    row_far_delta = head_sums(g_row.astype(F32) * row_far_out)
    log_col, delta_col, _, _ = combine(
        dot(stat, sum_second), dot(stat, sum_third), far_total, own_delta
    )
    log_row, delta_row, near_weight, far_weight = combine(
        near_total, near_delta, dot(stat, sum_first), row_far_delta
    )

    def backward(scores, q_stack, g_stack, grad, log_spread, delta_spread):
        prob = jnp.exp(scores - columns(log_spread)).astype(BF16)
        step = (prob.astype(F32) * (grad - columns(delta_spread)) * scale).astype(BF16)
        return fold(dot(step, keys)), dot_at(step, q_stack), dot_at(prob, g_stack)

    dq_col, dk_more, dv_more = backward(
        scores_col, q_stack_col, g_stack_col, product_col, log_col, delta_col
    )
    dq_row, dk_part, dv_part = backward(
        scores_row, q_stack_row, g_stack_row, product_row, log_row, delta_row
    )
    dk_all, dv_all = dk_part + dk_more, dv_part + dv_more
    exchange_start(
        3, s4, r4, wide([dq_col.astype(BF16), dk_all[rows:].astype(BF16), dv_all[rows:].astype(BF16)])
    )
    attended = (near_out * near_weight + row_far_out * far_weight).astype(BF16)

    part = dot(dot(spread_rows, attended).astype(BF16), w_ref[...])
    part_rows = planes * RH
    layer_copies = []
    for d in range(1, groups):
        piece = part[d * part_rows : (d + 1) * part_rows]
        part_out[d - 1] = piece.reshape(planes, RH, width).astype(BF16)
        copy = pltpu.make_async_remote_copy(
            src_ref=part_out.at[d - 1],
            dst_ref=part_in.at[d - 1],
            send_sem=head_send.at[1, d - 1],
            recv_sem=head_recv.at[1, d - 1],
            device_id={"head": lax.rem(mine - d + groups, groups)},
            device_id_type=MESH,
        )
        copy.start()
        layer_copies.append(copy)

    total = part[:part_rows]
    for d in range(1, groups):
        layer_copies[d - 1].wait_recv()
        total = total + part_in[d - 1].astype(F32).reshape(part_rows, width)
    layer_ref[0] = total.reshape(planes, RH, width).astype(BF16)
    for copy in head_copies + layer_copies:
        copy.wait_send()
    exchange_end(0, s1, r1)
    exchange_end(1, s2, r2)
    exchange_end(2, s3, r3)

    back_q, back_k, back_v = unwide(exchange_wait(3, s4, r4))
    dq_ref[0] = (dq_row + back_q).astype(BF16).reshape(planes, R, F)
    dk_ref[0] = (dk_all[:rows] + back_k).astype(BF16).reshape(planes, R, F)
    dv_ref[0] = (dv_all[:rows] + back_v).astype(BF16).reshape(planes, R, F)
    exchange_end(3, s4, r4)


def store_kernel(*refs):
    sources, targets, sem = refs[:4], refs[4:8], refs[8]
    copies = [
        pltpu.make_async_copy(src, dst, sem.at[at])
        for at, (src, dst) in enumerate(zip(sources, targets))
    ]
    for copy in copies:
        copy.start()
    for copy in copies:
        copy.wait()


def solution(mesh):
    n, groups = mesh.shape["band"], mesh.shape["head"]

    def body(queries, attn_keys, attn_values, out_proj, grad_out, plane_axes):
        _, planes, R, F = queries.shape
        width = out_proj.shape[1]
        whole = pl.BlockSpec(memory_space=pl.ANY)
        vmem = pl.BlockSpec(memory_space=pltpu.VMEM)
        wide = pltpu.VMEM((R * CHUNK, F), BF16)
        narrow = pltpu.VMEM((R * CHUNK, F // 2), BF16)
        part = pltpu.VMEM((groups - 1, planes, R // groups, width), BF16)
        shapes = [grad_out.shape] + [queries.shape] * 3
        results = pl.pallas_call(
            functools.partial(kernel, n, groups),
            out_shape=tuple(pltpu.VMEM(shape, BF16) for shape in shapes),
            in_specs=[whole] * 6,
            out_specs=(vmem,) * 4,
            scratch_shapes=[
                pltpu.VMEM(queries.shape, BF16),
                pltpu.VMEM(queries.shape, BF16),
                pltpu.VMEM(queries.shape, BF16),
                pltpu.VMEM(out_proj.shape, BF16),
                pltpu.VMEM(grad_out.shape, BF16),
                pltpu.SMEM(plane_axes.shape[::-1], I32),
                wide, wide, narrow, narrow, narrow, narrow, wide, wide, part, part, part,
                pltpu.SemaphoreType.DMA((4,)),
                pltpu.SemaphoreType.DMA((4,)),
                pltpu.SemaphoreType.DMA((2, groups - 1)),
                pltpu.SemaphoreType.DMA((2, groups - 1)),
                pltpu.SemaphoreType.DMA((6,)),
            ],
            compiler_params=pltpu.CompilerParams(
                collective_id=0, has_side_effects=True, vmem_limit_bytes=56 * 1024 * 1024
            ),
        )(queries, attn_keys, attn_values, out_proj, grad_out, plane_axes.T)
        return pl.pallas_call(
            store_kernel,
            out_shape=tuple(jax.ShapeDtypeStruct(shape, BF16) for shape in shapes),
            in_specs=[vmem] * 4,
            out_specs=(whole,) * 4,
            scratch_shapes=[pltpu.SemaphoreType.DMA((4,))],
        )(*[pltpu.with_memory_space_constraint(r, pltpu.VMEM) for r in results])

    rows = P("band", None, None, "head")
    cols = P("band", None, "head", None)
    return jax.shard_map(
        body,
        mesh=mesh,
        in_specs=(rows, rows, rows, P("head", None), cols, P()),
        out_specs=(cols, rows, rows, rows),
        check_vma=False,
    )
```
